256 devices in a mesh: wide: 32 (over y_hi, z, core), narrow: 8 (over x, y_lo).
Axes of the slice: x: 4, y: 4 (y_hi: 2, y_lo: 2; y = y_hi * 2 + y_lo), z: 8, core: 2. Of those that a mesh axis runs over, the one named last changes fastest.
Arguments:
- matrix: float32 [16384, 16384], P('narrow', 'wide'), may hold values from -64 to 64
Outputs:
- rotated: float32 [16384, 16384], P('narrow', 'wide')
The draws below stay inside these ranges and needn't reach their ends.
All inputs are finite; a program needn't handle non-finite values.
Results may differ from the reference program's by a relative error of at most 0.0003.
Values sent between devices are 32-bit elements; how exact they have to be, the bound alone decides.
No kernel may reach another device: no remote copies, remote signals or barrier semaphores. Data moves between devices by JAX's collectives and lax.ppermute only.
A program may use at most 64 MiB of HBM per device.

```python
import math
import jax
import jax.numpy as jnp
from jax import lax

B = 256
STEPS = 2
N = 16384
N_WIDE = 32


def draw_matrix(key, part):
    subkeys = jax.random.split(jax.random.fold_in(key, 7), 3)
    row_scale = jnp.exp(jax.random.uniform(subkeys[0], (N,), jnp.float32, math.log(0.3), math.log(3.0)))
    col_scale = jnp.exp(jax.random.uniform(subkeys[1], (N,), jnp.float32, math.log(0.3), math.log(3.0)))
    base_values = jnp.clip(jax.random.normal(subkeys[2], (N, N), jnp.float32), -6.0, 6.0)
    return (base_values * row_scale[:, None] * col_scale[None, :]).astype(jnp.float32)


def setup_inputs(seed: int = 0) -> dict:
    key_list = jax.random.split(jax.random.key(seed), 2)
    return {
        "matrix": draw_matrix(jax.random.fold_in(key_list[1], 71), 0),
    }


def product(left, right):
    return jnp.dot(left, right, precision=lax.Precision.HIGHEST)

def spd_solve(factor_low, right_side):
    first_pass = lax.linalg.triangular_solve(factor_low, right_side, left_side=True, lower=True)
    return lax.linalg.triangular_solve(factor_low, first_pass, left_side=True, lower=True, transpose_a=True)

def turn_pair(upper_block, lower_block, cross_gram, upper_norms, lower_norms):
    damped = cross_gram / (upper_norms[:, None] + lower_norms[None, :])
    block_width = damped.shape[0]
    identity = jnp.eye(block_width, dtype=damped.dtype)
    left_square = product(damped, damped.T)
    left_factor = jnp.linalg.cholesky(identity + left_square)
    solved = spd_solve(left_factor, jnp.concatenate([identity, damped], axis=1))
    inverse = solved[:, :block_width]
    inverse_damped = solved[:, block_width:]
    keep_upper = 2.0 * inverse - identity
    into_lower = 2.0 * inverse_damped
    into_upper = -2.0 * inverse_damped.T
    keep_lower = identity - 2.0 * product(damped.T, inverse_damped)
    new_upper = product(upper_block, keep_upper) + product(lower_block, into_upper)
    new_lower = product(upper_block, into_lower) + product(lower_block, keep_lower)
    return (new_upper, new_lower)

def rotate_whole(blocks):
    upper_block, lower_block = blocks
    cross_gram = product(upper_block.T, lower_block)
    upper_norms = jnp.sum(upper_block * upper_block, axis=0)
    lower_norms = jnp.sum(lower_block * lower_block, axis=0)
    return turn_pair(upper_block, lower_block, cross_gram, upper_norms, lower_norms)

def reference(matrix):
    order_rows = matrix.shape[0]
    paired = matrix.reshape(order_rows, N_WIDE, 2, B)
    uppers = jnp.transpose(paired[:, :, 0, :], (1, 0, 2))
    lowers = jnp.transpose(paired[:, :, 1, :], (1, 0, 2))
    for step_index in range(STEPS):
        uppers, lowers = lax.map(rotate_whole, (uppers, lowers))
        lowers = jnp.roll(lowers, 1, axis=0)
    joined = jnp.stack([uppers, lowers], axis=2)
    return jnp.transpose(joined, (1, 0, 2, 3)).reshape(order_rows, order_rows)
```

```python
import functools

import jax
import jax.numpy as jnp
from jax import lax
from jax.experimental import pallas as pl
from jax.experimental.pallas import tpu as pltpu
from jax.sharding import PartitionSpec as P

PIECES = 4
MEMBERS = 8
TAIL = 8
ROUNDS = (1, 2, 6)
F32 = jnp.float32
BF16 = jnp.bfloat16
PLAIN = (((1,), (0,)), ((), ()))
ROWS_FIRST = (((0,), (0,)), ((), ()))
COLS_LAST = (((1,), (1,)), ((), ()))
VMEM = pl.BlockSpec(memory_space=pltpu.VMEM)
MIB = 1 << 20


def halves(value):
    high = value.astype(BF16)
    return high, (value - high.astype(F32)).astype(BF16)


def dot(left, right, dims=PLAIN):
    return lax.dot_general(left, right, dims, preferred_element_type=F32)


def exact(left, right, dims=PLAIN):
    return lax.dot_general(
        left, right, dims, precision=lax.Precision.HIGHEST, preferred_element_type=F32
    )


def part_of(upper, lower):
    upper_high, upper_low = halves(upper)
    lower_high, lower_low = halves(lower)
    cross = dot(upper_high, lower_high, ROWS_FIRST)
    cross += dot(upper_high, lower_low, ROWS_FIRST)
    cross += dot(upper_low, lower_high, ROWS_FIRST)
    width = upper.shape[1]
    row = lax.broadcasted_iota(jnp.int32, (TAIL, width), 0)
    norms = jnp.where(row == 0, jnp.sum(upper * upper, axis=0, keepdims=True), 0.0)
    norms = jnp.where(row == 1, jnp.sum(lower * lower, axis=0, keepdims=True), norms)
    return cross, norms


def first_gram_body(upper_ref, lower_ref, out_ref):
    width = upper_ref.shape[1]
    cross, norms = part_of(upper_ref[...], lower_ref[...])

    @pl.when(pl.program_id(0) == 0)
    def _():
        out_ref[:width] = cross
        out_ref[width:] = norms

    @pl.when(pl.program_id(0) > 0)
    def _():
        out_ref[:width] += cross
        out_ref[width:] += norms


def first_gram(matrix, tile=1024):
    rows, width = matrix.shape[0], matrix.shape[1] // 2
    return pl.pallas_call(
        first_gram_body,
        grid=(rows // tile,),
        in_specs=[
            pl.BlockSpec((tile, width), lambda i: (i, 0)),
            pl.BlockSpec((tile, width), lambda i: (i, 1)),
        ],
        out_specs=pl.BlockSpec((width + TAIL, width), lambda i: (0, 0)),
        out_shape=jax.ShapeDtypeStruct((width + TAIL, width), F32),
        compiler_params=pltpu.CompilerParams(vmem_limit_bytes=8 * MIB),
        name="first_gram",
    )(matrix, matrix)


def gram_body(tile, count, upper_ref, *refs):
    lower_refs, out_ref = refs[:count], refs[-1]
    width = upper_ref.shape[1]
    start, total = 0, None
    for lower_ref in lower_refs:
        for at in range(0, lower_ref.shape[0], tile):
            part = part_of(upper_ref[pl.ds(start, tile), :], lower_ref[pl.ds(at, tile), :])
            total = part if total is None else tuple(a + b for a, b in zip(total, part))
            start += tile
    out_ref[:width], out_ref[width:] = total


def gram(upper, lowers, after=(), tile=512):
    width = upper.shape[1]
    return pl.pallas_call(
        functools.partial(gram_body, tile, len(lowers)),
        in_specs=[VMEM] * (1 + len(lowers)) + [pl.BlockSpec(memory_space=pl.ANY)] * len(after),
        out_specs=VMEM,
        out_shape=jax.ShapeDtypeStruct((width + TAIL, width), F32),
        compiler_params=pltpu.CompilerParams(vmem_limit_bytes=8 * MIB),
        name="gram",
    )(upper, *lowers, *after)


def solve_body(left_ref, right_ref, high_ref, low_ref, inverse_ref):
    width = left_ref.shape[1]
    cross = left_ref[:width] + right_ref[:width]
    norms = left_ref[width:] + right_ref[width:]
    row = lax.broadcasted_iota(jnp.int32, (width, width), 0)
    column = lax.broadcasted_iota(jnp.int32, (width, width), 1)
    identity = jnp.where(row == column, 1.0, 0.0).astype(F32)
    upper_norms = jnp.sum(jnp.where(row == column, norms[0:1], 0.0), axis=1, keepdims=True)
    damped = cross / (upper_norms + norms[1:2])
    square = exact(damped, damped, COLS_LAST)
    bound = jnp.max(jnp.sum(jnp.abs(square), axis=0))
    scale = 2.0 / (2.0 + bound)
    whole = identity + square
    inverse_ref[...] = scale * (2.0 * identity - scale * whole)

    def more(state):
        count, off = state
        return jnp.logical_and(count < 40, off > 1e-3)

    def refine(state):
        count, _ = state
        inverse = inverse_ref[...]
        rest = identity - exact(whole, inverse)
        inverse_ref[...] = inverse + exact(inverse, rest)
        return count + 1, jnp.max(jnp.sum(jnp.abs(rest), axis=0))

    lax.while_loop(more, refine, (jnp.int32(0), jnp.float32(1.0)))
    inverse = inverse_ref[...]
    into_lower = 2.0 * exact(inverse, damped)
    into_upper = -into_lower.T
    keep_lower = identity + exact(into_upper, damped)
    for place, block in (
        ((0, 0), 2.0 * inverse - identity),
        ((0, 1), into_lower),
        ((1, 0), into_upper),
        ((1, 1), keep_lower),
    ):
        high, low = halves(block)
        at = (pl.ds(place[0] * width, width), pl.ds(place[1] * width, width))
        high_ref[at] = high
        low_ref[at] = low


def solve(left, right):
    width = left.shape[1]
    out = jax.ShapeDtypeStruct((2 * width, 2 * width), BF16)
    return pl.pallas_call(
        solve_body,
        in_specs=[VMEM] * 2,
        out_specs=(VMEM, VMEM),
        out_shape=(out, out),
        scratch_shapes=[pltpu.VMEM((width, width), F32)],
        compiler_params=pltpu.CompilerParams(vmem_limit_bytes=8 * MIB),
        name="solve",
    )(left, right)


def turn_rows(block_refs, starts, high_ref, low_ref, side, at, tile):
    width = 256
    columns = pl.ds(side * width, width)
    total, depth = None, 0
    for ref, first in zip(block_refs, starts):
        high, low = halves(ref[pl.ds(first + at, tile), :])
        rows = pl.ds(depth, high.shape[1])
        turn_high, turn_low = high_ref[rows, columns], low_ref[rows, columns]
        part = dot(high, turn_high) + dot(low, turn_high) + dot(high, turn_low)
        total = part if total is None else total + part
        depth += high.shape[1]
    return total


def turn_body(side, starts, tile, *refs):
    *block_refs, high_ref, low_ref, out_ref = refs
    for at in range(0, out_ref.shape[0], tile):
        total = turn_rows(block_refs, starts, high_ref, low_ref, side, at, tile)
        out_ref[pl.ds(at, tile), :] = total


def turn(blocks, turns, side, starts, rows, tile=512):
    return pl.pallas_call(
        functools.partial(turn_body, side, starts, tile),
        in_specs=[VMEM] * (len(blocks) + 2),
        out_specs=VMEM,
        out_shape=jax.ShapeDtypeStruct((rows, 256), F32),
        compiler_params=pltpu.CompilerParams(vmem_limit_bytes=8 * MIB),
        name="turn_lower" if side else "turn_upper",
    )(*blocks, *turns)


def last_body(tile, flag_ref, upper_ref, *refs):
    *others, out_ref = refs
    half = len(others) // 2
    for want, sources in ((1, others[:half]), (0, others[half:])):

        @pl.when(flag_ref[0] == want)
        def _(sources=sources):
            *lower_refs, high_ref, low_ref = sources
            at = 0
            for lower_ref in lower_refs:
                for inner in range(0, lower_ref.shape[0], tile):
                    total = turn_rows(
                        (upper_ref, lower_ref), (at - inner, 0), high_ref, low_ref, 0, inner, tile
                    )
                    out_ref[pl.ds(at, tile), :256] = total
                    at += tile


def last_upper(flag, upper, near, turns_near, far, turns_far, tile=512):
    rows, width = upper.shape
    others = [*near, *turns_near, *far, *turns_far]
    return pl.pallas_call(
        functools.partial(last_body, tile),
        in_specs=[pl.BlockSpec(memory_space=pltpu.SMEM)] + [VMEM] * (1 + len(others)),
        out_specs=VMEM,
        out_shape=jax.ShapeDtypeStruct((rows, 2 * width), F32),
        compiler_params=pltpu.CompilerParams(vmem_limit_bytes=8 * MIB),
        name="last_upper",
    )(flag, upper, *others)


def move(value, target):
    wide, narrow = lax.axis_size("wide"), lax.axis_size("narrow")
    pairs = []
    for w in range(wide):
        for n in range(narrow):
            to = target(w, n)
            if to is not None:
                pairs.append((w * narrow + n, (to[0] % wide) * narrow + to[1]))
    return lax.ppermute(value, ("wide", "narrow"), pairs)


def all_sum(value, active=None):
    for k, mask in enumerate(ROUNDS):
        other = move(
            value, lambda w, n: (w, n ^ mask if active is None or w % 2 == active else n)
        )
        if k + 1 == len(ROUNDS):
            return value, other
        value = value + other


def within(w, n):
    return w ^ 1, n


def across(w, n):
    return (w + 1 if w % 2 else w - 1), n


def to_odd(w, n):
    return None if w % 2 else (w + 1, n)


def to_even(w, n):
    return (w + 1, n) if w % 2 else None


def last_one_body(tile, upper_ref, *refs):
    *lower_refs, high_ref, low_ref, out_ref = refs
    at = 0
    for lower_ref in lower_refs:
        for inner in range(0, lower_ref.shape[0], tile):
            total = turn_rows((upper_ref, lower_ref), (at - inner, 0), high_ref, low_ref, 0, inner, tile)
            out_ref[pl.ds(at, tile), :256] = total
            at += tile


def last_one(upper, lowers, turns, tile=512):
    rows, width = upper.shape
    others = [*lowers, *turns]
    return pl.pallas_call(
        functools.partial(last_one_body, tile),
        in_specs=[VMEM] * (1 + len(others)),
        out_specs=VMEM,
        out_shape=jax.ShapeDtypeStruct((rows, 2 * width), F32),
        compiler_params=pltpu.CompilerParams(vmem_limit_bytes=8 * MIB),
        name="last_upper",
    )(upper, *others)


def onward(w, n):
    return w + 1, n


def shards(matrix):
    rows, width = matrix.shape[0], matrix.shape[1] // 2
    piece = rows // PIECES
    starts = [k * piece for k in range(PIECES)]
    turns = solve(*all_sum(first_gram(matrix)))
    lowers = [move(turn([matrix], turns, 1, (at,), piece), onward) for at in starts]
    upper = turn([matrix], turns, 0, (0,), rows)
    turns = solve(*all_sum(gram(upper, lowers)))
    last = [
        move(turn([upper, lowers[k]], turns, 1, (at, 0), piece), onward)
        for k, at in enumerate(starts)
    ]
    out = last_one(upper, lowers, turns)
    for k, at in enumerate(starts):
        out = lax.dynamic_update_slice(out, last[k], (at, width))
    return out


def solution(mesh):
    spec = P("narrow", "wide")
    return jax.shard_map(shards, mesh=mesh, in_specs=(spec,), out_specs=spec, check_vma=False)
```

```python
import functools

import jax
import jax.numpy as jnp
from jax import lax
from jax.experimental import pallas as pl
from jax.experimental.pallas import tpu as pltpu
from jax.sharding import PartitionSpec as P

PIECES = 2
LAST_PIECES = 2
TAIL = 8
ROUNDS = (1, 2, 6)
F32 = jnp.float32
BF16 = jnp.bfloat16
PLAIN = (((1,), (0,)), ((), ()))
ROWS_FIRST = (((0,), (0,)), ((), ()))
COLS_LAST = (((1,), (1,)), ((), ()))
VMEM = pl.BlockSpec(memory_space=pltpu.VMEM)
MIB = 1 << 20


def halves(value):
    high = value.astype(BF16)
    return high, (value - high.astype(F32)).astype(BF16)


def dot(left, right, dims=PLAIN):
    return lax.dot_general(left, right, dims, preferred_element_type=F32)


def exact(left, right, dims=PLAIN):
    return lax.dot_general(
        left, right, dims, precision=lax.Precision.HIGHEST, preferred_element_type=F32
    )


def part_of(upper, lower):
    upper_high, upper_low = halves(upper)
    lower_high, lower_low = halves(lower)
    cross = dot(upper_high, lower_high, ROWS_FIRST)
    cross += dot(upper_high, lower_low, ROWS_FIRST)
    cross += dot(upper_low, lower_high, ROWS_FIRST)
    width = upper.shape[1]
    row = lax.broadcasted_iota(jnp.int32, (TAIL, width), 0)
    norms = jnp.where(row == 0, jnp.sum(upper * upper, axis=0, keepdims=True), 0.0)
    norms = jnp.where(row == 1, jnp.sum(lower * lower, axis=0, keepdims=True), norms)
    return cross, norms


def first_gram_body(tile, matrix_ref, out_ref, block_ref, sems):
    rows, width = block_ref.shape[0], out_ref.shape[1]
    copies = []
    for k in range(rows // tile):
        part = pl.ds(k * tile, tile)
        copies.append(
            pltpu.make_async_copy(matrix_ref.at[part, :], block_ref.at[part, :], sems.at[k])
        )
        copies[-1].start()
    total = None
    for k, copy in enumerate(copies):
        copy.wait()
        at = pl.ds(k * tile, tile)
        part = part_of(block_ref[at, :width], block_ref[at, width:])
        total = part if total is None else tuple(a + b for a, b in zip(total, part))
    out_ref[:width], out_ref[width:] = total


def first_gram(matrix, tile=512):
    rows, width = matrix.shape[0], matrix.shape[1] // 2
    return pl.pallas_call(
        functools.partial(first_gram_body, tile),
        in_specs=[pl.BlockSpec(memory_space=pltpu.HBM)],
        out_specs=(VMEM, VMEM),
        out_shape=(
            jax.ShapeDtypeStruct((width + TAIL, width), F32),
            jax.ShapeDtypeStruct(matrix.shape, F32),
        ),
        scratch_shapes=[pltpu.SemaphoreType.DMA((rows // tile,))],
        compiler_params=pltpu.CompilerParams(vmem_limit_bytes=16 * MIB),
        name="first_gram",
    )(matrix)


def gram_body(tile, count, upper_ref, *refs):
    lower_refs, out_ref = refs[:count], refs[-1]
    width = upper_ref.shape[1]
    start, total = 0, None
    for lower_ref in lower_refs:
        for at in range(0, lower_ref.shape[0], tile):
            part = part_of(upper_ref[pl.ds(start, tile), :], lower_ref[pl.ds(at, tile), :])
            total = part if total is None else tuple(a + b for a, b in zip(total, part))
            start += tile
    out_ref[:width], out_ref[width:] = total


def gram(upper, lowers, tile=512):
    width = upper.shape[1]
    return pl.pallas_call(
        functools.partial(gram_body, tile, len(lowers)),
        in_specs=[VMEM] * (1 + len(lowers)),
        out_specs=VMEM,
        out_shape=jax.ShapeDtypeStruct((width + TAIL, width), F32),
        compiler_params=pltpu.CompilerParams(vmem_limit_bytes=8 * MIB),
        name="gram",
    )(upper, *lowers)


def split_dot(left, right):
    return dot(left[0], right[0]) + (dot(left[0], right[1]) + dot(left[1], right[0]))


def solve_body(left_ref, right_ref, high_ref, low_ref, inverse_ref):
    width = left_ref.shape[1]
    cross = left_ref[:width] + right_ref[:width]
    norms = left_ref[width:] + right_ref[width:]
    row = lax.broadcasted_iota(jnp.int32, (width, width), 0)
    column = lax.broadcasted_iota(jnp.int32, (width, width), 1)
    identity = jnp.where(row == column, 1.0, 0.0).astype(F32)
    upper_norms = jnp.sum(jnp.where(row == column, norms[0:1], 0.0), axis=1, keepdims=True)
    damped = cross / (upper_norms + norms[1:2])
    square = exact(damped, damped, COLS_LAST)
    bound = jnp.max(jnp.sum(jnp.abs(square), axis=0))
    scale = 2.0 / (2.0 + bound)
    whole = identity + square
    rest = identity - scale * whole
    rest_halves = halves(rest)
    second = split_dot(rest_halves, rest_halves)
    third = split_dot(rest_halves, halves(second))
    inverse_ref[...] = scale * (identity + (rest + (second + third)))

    def more(state):
        count, off = state
        return jnp.logical_and(count < 40, off > 1e-3)

    def refine(state):
        count, _ = state
        inverse = inverse_ref[...]
        rest = identity - exact(whole, inverse)
        inverse_ref[...] = inverse + exact(inverse, rest)
        return count + 1, jnp.max(jnp.sum(jnp.abs(rest), axis=0))

    near_one = bound / (2.0 + bound)
    lax.while_loop(more, refine, (jnp.int32(0), near_one * near_one))
    inverse = inverse_ref[...]
    damped_halves = halves(damped)
    into_lower = 2.0 * split_dot(halves(inverse), damped_halves)
    into_upper = -into_lower.T
    into_upper_halves = halves(into_upper)
    keep_lower = identity + split_dot(into_upper_halves, damped_halves)
    for place, (high, low) in (
        ((0, 0), halves(2.0 * inverse - identity)),
        ((0, 1), halves(into_lower)),
        ((1, 0), into_upper_halves),
        ((1, 1), halves(keep_lower)),
    ):
        at = (pl.ds(place[0] * width, width), pl.ds(place[1] * width, width))
        high_ref[at] = high
        low_ref[at] = low


def solve(left, right):
    width = left.shape[1]
    out = jax.ShapeDtypeStruct((2 * width, 2 * width), BF16)
    return pl.pallas_call(
        solve_body,
        in_specs=[VMEM] * 2,
        out_specs=(VMEM, VMEM),
        out_shape=(out, out),
        scratch_shapes=[pltpu.VMEM((width, width), F32)],
        compiler_params=pltpu.CompilerParams(vmem_limit_bytes=8 * MIB),
        name="solve",
    )(left, right)


def turn_rows(block_refs, starts, high_ref, low_ref, side, at, tile):
    width = 256
    columns = pl.ds(side * width, width)
    total, depth = None, 0
    for ref, first in zip(block_refs, starts):
        high, low = halves(ref[pl.ds(first + at, tile), :])
        rows = pl.ds(depth, high.shape[1])
        turn_high, turn_low = high_ref[rows, columns], low_ref[rows, columns]
        part = dot(high, turn_high) + dot(low, turn_high) + dot(high, turn_low)
        total = part if total is None else total + part
        depth += high.shape[1]
    return total


def turn_body(side, starts, tile, *refs):
    *block_refs, high_ref, low_ref, out_ref = refs
    if starts is None:
        at = 0
        for lower_ref in block_refs[1:]:
            for inner in range(0, lower_ref.shape[0], tile):
                out_ref[pl.ds(at, tile), :] = turn_rows(
                    (block_refs[0], lower_ref), (at - inner, 0), high_ref, low_ref, side, inner, tile
                )
                at += tile
        return
    for at in range(0, out_ref.shape[0], tile):
        total = turn_rows(block_refs, starts, high_ref, low_ref, side, at, tile)
        out_ref[pl.ds(at, tile), :] = total


def turn(blocks, turns, side, starts, rows, tile=512):
    return pl.pallas_call(
        functools.partial(turn_body, side, starts, tile),
        in_specs=[VMEM] * (len(blocks) + 2),
        out_specs=VMEM,
        out_shape=jax.ShapeDtypeStruct((rows, 256), F32),
        compiler_params=pltpu.CompilerParams(vmem_limit_bytes=8 * MIB),
        name="turn_lower" if side else "turn_upper",
    )(*blocks, *turns)


def last_body(tile, count, flag_ref, done_ref, upper_ref, *refs):
    lower_refs, (high_ref, low_ref) = refs[:count], refs[count : count + 2]
    piece_refs, out_ref = refs[count + 2 : 2 * count + 2], refs[2 * count + 2]
    stage_ref, sem = refs[2 * count + 3 :]
    width = upper_ref.shape[1]
    columns = out_ref.at[:, pl.ds(0, width)]

    @pl.when(flag_ref[0] == 1)
    def _():
        fetch = pltpu.make_async_copy(done_ref, stage_ref, sem)
        fetch.start()
        fetch.wait()

    @pl.when(flag_ref[0] == 0)
    def _():
        at = 0
        for lower_ref, piece_ref in zip(lower_refs, piece_refs):
            for inner in range(0, lower_ref.shape[0], tile):
                blocks, starts = (upper_ref, lower_ref), (at - inner, 0)
                stage_ref[pl.ds(at, tile), :] = turn_rows(
                    blocks, starts, high_ref, low_ref, 0, inner, tile
                )
                piece_ref[pl.ds(inner, tile), :] = turn_rows(
                    blocks, starts, high_ref, low_ref, 1, inner, tile
                )
                at += tile

    copy = pltpu.make_async_copy(stage_ref, columns, sem)
    copy.start()
    copy.wait()


def last_turn(flag, done, upper, far, turns_far, tile=512):
    rows, width = upper.shape
    everywhere = pl.BlockSpec(memory_space=pl.ANY)
    *pieces, out = pl.pallas_call(
        functools.partial(last_body, tile, len(far)),
        in_specs=[pl.BlockSpec(memory_space=pltpu.SMEM)] + [VMEM] * (4 + len(far)),
        out_specs=(*[VMEM] * len(far), everywhere),
        out_shape=(
            *[jax.ShapeDtypeStruct(piece.shape, F32) for piece in far],
            jax.ShapeDtypeStruct((rows, 2 * width), F32),
        ),
        scratch_shapes=[pltpu.VMEM((rows, width), F32), pltpu.SemaphoreType.DMA],
        compiler_params=pltpu.CompilerParams(vmem_limit_bytes=8 * MIB),
        name="last_turn",
    )(flag, done, upper, *far, *turns_far)
    return pieces, out


def finish_body(count, flag_ref, before_ref, *refs):
    near_refs, far_refs, out_ref = refs[:count], refs[count : 2 * count], refs[2 * count]
    stage_ref, in_sems, out_sems = refs[2 * count + 1 :]
    width = stage_ref.shape[1]
    for want, sources in ((1, near_refs), (0, far_refs)):

        @pl.when(flag_ref[0] == want)
        def _(sources=sources):
            at, spans, fetches, puts = 0, [], [], []
            for k, source in enumerate(sources):
                spans.append(pl.ds(at, source.shape[0]))
                fetches.append(
                    pltpu.make_async_copy(source, stage_ref.at[spans[k], :], in_sems.at[k])
                )
                fetches[k].start()
                at += source.shape[0]
            for k, span in enumerate(spans):
                fetches[k].wait()
                place = out_ref.at[span, pl.ds(width, width)]
                puts.append(pltpu.make_async_copy(stage_ref.at[span, :], place, out_sems.at[k]))
                puts[k].start()
            for put in puts:
                put.wait()


def finish(flag, out, near, far):
    rows, width = out.shape[0], out.shape[1] // 2
    everywhere = pl.BlockSpec(memory_space=pl.ANY)
    count = len(near)
    return pl.pallas_call(
        functools.partial(finish_body, count),
        in_specs=[pl.BlockSpec(memory_space=pltpu.SMEM)] + [everywhere] * (1 + 2 * count),
        out_specs=everywhere,
        out_shape=jax.ShapeDtypeStruct(out.shape, F32),
        scratch_shapes=[
            pltpu.VMEM((rows, width), F32),
            pltpu.SemaphoreType.DMA((count,)),
            pltpu.SemaphoreType.DMA((count,)),
        ],
        input_output_aliases={1: 0},
        compiler_params=pltpu.CompilerParams(vmem_limit_bytes=8 * MIB),
        name="finish",
    )(flag, out, *near, *far)


def move(value, target):
    wide, narrow = lax.axis_size("wide"), lax.axis_size("narrow")
    pairs = []
    for w in range(wide):
        for n in range(narrow):
            to = target(w, n)
            if to is not None:
                pairs.append((w * narrow + n, (to[0] % wide) * narrow + to[1]))
    return lax.ppermute(value, ("wide", "narrow"), pairs)


def all_sum(value, active=None, rounds=ROUNDS):
    for k, mask in enumerate(rounds):
        other = move(
            value, lambda w, n: (w, n ^ mask if active is None or w % 2 == active else n)
        )
        if k + 1 == len(rounds):
            return value, other
        value = value + other


def within(w, n):
    return w ^ 1, n


def onward(w, n):
    return w + 1, n


def shards(matrix):
    rows = matrix.shape[0]
    piece, small = rows // PIECES, rows // LAST_PIECES
    starts = [k * piece for k in range(PIECES)]
    last_starts = [k * small for k in range(LAST_PIECES)]
    flag = (lax.axis_index("wide") & 1).astype(jnp.int32).reshape(1)
    parts, matrix = first_gram(matrix)
    turns = solve(*all_sum(parts))
    near, far = [], []
    for at in starts:
        lower = turn([matrix], turns, 1, (at,), piece)
        near.append(move(lower, within))
        far.append(move(lower, onward))
    upper = turn([matrix], turns, 0, (0,), rows)
    turns = solve(*all_sum(gram(upper, near), 1, (2, 6, 1)))
    after = [
        turn([upper, near[at // piece]], turns, 1, (at, at % piece), small)
        for at in last_starts
    ]
    done = turn([upper, *near], turns, 0, None, rows)
    last_far = [move(lower, onward) for lower in after]
    parts = gram(upper, far)
    parts = parts + move(parts, lambda w, n: (w, n if w % 2 else n ^ 1))
    parts = all_sum(parts, 0, (2, 6))
    turns = solve(*parts)
    pieces, out = last_turn(flag, done, upper, far, turns)
    last_near = [move(lower, within) for lower in pieces]
    return finish(flag, out, last_near, last_far)


def solution(mesh):
    spec = P("narrow", "wide")

    return jax.shard_map(shards, mesh=mesh, in_specs=(spec,), out_specs=spec, check_vma=False)
```

```python
import functools

import jax
import jax.numpy as jnp
from jax import lax
from jax.experimental import pallas as pl
from jax.experimental.pallas import tpu as pltpu
from jax.sharding import PartitionSpec as P

PIECES = 2
LAST_PIECES = 2
TAIL = 8
ROUNDS = (1, 2, 6)
F32 = jnp.float32
BF16 = jnp.bfloat16
PLAIN = (((1,), (0,)), ((), ()))
ROWS_FIRST = (((0,), (0,)), ((), ()))
COLS_LAST = (((1,), (1,)), ((), ()))
VMEM = pl.BlockSpec(memory_space=pltpu.VMEM)
MIB = 1 << 20


def halves(value):
    high = value.astype(BF16)
    return high, (value - high.astype(F32)).astype(BF16)


def dot(left, right, dims=PLAIN):
    return lax.dot_general(left, right, dims, preferred_element_type=F32)


def exact(left, right, dims=PLAIN):
    return lax.dot_general(
        left, right, dims, precision=lax.Precision.HIGHEST, preferred_element_type=F32
    )


def part_of(upper, lower):
    upper_high, upper_low = halves(upper)
    lower_high, lower_low = halves(lower)
    cross = dot(upper_high, lower_high, ROWS_FIRST)
    cross += dot(upper_high, lower_low, ROWS_FIRST)
    cross += dot(upper_low, lower_high, ROWS_FIRST)
    width = upper.shape[1]
    row = lax.broadcasted_iota(jnp.int32, (TAIL, width), 0)
    norms = jnp.where(row == 0, jnp.sum(upper * upper, axis=0, keepdims=True), 0.0)
    norms = jnp.where(row == 1, jnp.sum(lower * lower, axis=0, keepdims=True), norms)
    return cross, norms


def first_gram_body(upper_ref, lower_ref, out_ref):
    width = upper_ref.shape[1]
    cross, norms = part_of(upper_ref[...], lower_ref[...])

    @pl.when(pl.program_id(0) == 0)
    def _():
        out_ref[:width] = cross
        out_ref[width:] = norms

    @pl.when(pl.program_id(0) > 0)
    def _():
        out_ref[:width] += cross
        out_ref[width:] += norms


def first_gram(matrix, tile=1024):
    rows, width = matrix.shape[0], matrix.shape[1] // 2
    return pl.pallas_call(
        first_gram_body,
        grid=(rows // tile,),
        in_specs=[
            pl.BlockSpec((tile, width), lambda i: (i, 0)),
            pl.BlockSpec((tile, width), lambda i: (i, 1)),
        ],
        out_specs=pl.BlockSpec((width + TAIL, width), lambda i: (0, 0)),
        out_shape=jax.ShapeDtypeStruct((width + TAIL, width), F32),
        compiler_params=pltpu.CompilerParams(vmem_limit_bytes=8 * MIB),
        name="first_gram",
    )(matrix, matrix)


def gram_body(tile, count, upper_ref, *refs):
    lower_refs, out_ref = refs[:count], refs[-1]
    width = upper_ref.shape[1]
    start, total = 0, None
    for lower_ref in lower_refs:
        for at in range(0, lower_ref.shape[0], tile):
            part = part_of(upper_ref[pl.ds(start, tile), :], lower_ref[pl.ds(at, tile), :])
            total = part if total is None else tuple(a + b for a, b in zip(total, part))
            start += tile
    out_ref[:width], out_ref[width:] = total


def gram(upper, lowers, tile=512):
    width = upper.shape[1]
    return pl.pallas_call(
        functools.partial(gram_body, tile, len(lowers)),
        in_specs=[VMEM] * (1 + len(lowers)),
        out_specs=VMEM,
        out_shape=jax.ShapeDtypeStruct((width + TAIL, width), F32),
        compiler_params=pltpu.CompilerParams(vmem_limit_bytes=8 * MIB),
        name="gram",
    )(upper, *lowers)


def split_dot(left, right):
    return dot(left[0], right[0]) + (dot(left[0], right[1]) + dot(left[1], right[0]))


def solve_body(left_ref, right_ref, high_ref, low_ref, inverse_ref):
    width = left_ref.shape[1]
    cross = left_ref[:width] + right_ref[:width]
    norms = left_ref[width:] + right_ref[width:]
    row = lax.broadcasted_iota(jnp.int32, (width, width), 0)
    column = lax.broadcasted_iota(jnp.int32, (width, width), 1)
    identity = jnp.where(row == column, 1.0, 0.0).astype(F32)
    upper_norms = jnp.sum(jnp.where(row == column, norms[0:1], 0.0), axis=1, keepdims=True)
    damped = cross / (upper_norms + norms[1:2])
    square = exact(damped, damped, COLS_LAST)
    bound = jnp.max(jnp.sum(jnp.abs(square), axis=0))
    scale = 2.0 / (2.0 + bound)
    whole = identity + square
    rest = identity - scale * whole
    rest_halves = halves(rest)
    second = split_dot(rest_halves, rest_halves)
    third = split_dot(rest_halves, halves(second))
    inverse_ref[...] = scale * (identity + (rest + (second + third)))

    def more(state):
        count, off = state
        return jnp.logical_and(count < 40, off > 1e-3)

    def refine(state):
        count, _ = state
        inverse = inverse_ref[...]
        rest = identity - exact(whole, inverse)
        inverse_ref[...] = inverse + exact(inverse, rest)
        return count + 1, jnp.max(jnp.sum(jnp.abs(rest), axis=0))

    near_one = bound / (2.0 + bound)
    lax.while_loop(more, refine, (jnp.int32(0), near_one * near_one))
    inverse = inverse_ref[...]
    damped_halves = halves(damped)
    into_lower = 2.0 * split_dot(halves(inverse), damped_halves)
    into_upper = -into_lower.T
    into_upper_halves = halves(into_upper)
    keep_lower = identity + split_dot(into_upper_halves, damped_halves)
    for place, (high, low) in (
        ((0, 0), halves(2.0 * inverse - identity)),
        ((0, 1), halves(into_lower)),
        ((1, 0), into_upper_halves),
        ((1, 1), halves(keep_lower)),
    ):
        at = (pl.ds(place[0] * width, width), pl.ds(place[1] * width, width))
        high_ref[at] = high
        low_ref[at] = low


def solve(left, right):
    width = left.shape[1]
    out = jax.ShapeDtypeStruct((2 * width, 2 * width), BF16)
    return pl.pallas_call(
        solve_body,
        in_specs=[VMEM] * 2,
        out_specs=(VMEM, VMEM),
        out_shape=(out, out),
        scratch_shapes=[pltpu.VMEM((width, width), F32)],
        compiler_params=pltpu.CompilerParams(vmem_limit_bytes=8 * MIB),
        name="solve",
    )(left, right)


def turn_rows(block_refs, starts, high_ref, low_ref, side, at, tile):
    width = 256
    columns = pl.ds(side * width, width)
    total, depth = None, 0
    for ref, first in zip(block_refs, starts):
        high, low = halves(ref[pl.ds(first + at, tile), :])
        rows = pl.ds(depth, high.shape[1])
        turn_high, turn_low = high_ref[rows, columns], low_ref[rows, columns]
        part = dot(high, turn_high) + dot(low, turn_high) + dot(high, turn_low)
        total = part if total is None else total + part
        depth += high.shape[1]
    return total


def turn_body(side, starts, tile, *refs):
    *block_refs, high_ref, low_ref, out_ref = refs
    if starts is None:
        at = 0
        for lower_ref in block_refs[1:]:
            for inner in range(0, lower_ref.shape[0], tile):
                out_ref[pl.ds(at, tile), :] = turn_rows(
                    (block_refs[0], lower_ref), (at - inner, 0), high_ref, low_ref, side, inner, tile
                )
                at += tile
        return
    for at in range(0, out_ref.shape[0], tile):
        total = turn_rows(block_refs, starts, high_ref, low_ref, side, at, tile)
        out_ref[pl.ds(at, tile), :] = total


def turn(blocks, turns, side, starts, rows, tile=512):
    return pl.pallas_call(
        functools.partial(turn_body, side, starts, tile),
        in_specs=[VMEM] * (len(blocks) + 2),
        out_specs=VMEM,
        out_shape=jax.ShapeDtypeStruct((rows, 256), F32),
        compiler_params=pltpu.CompilerParams(vmem_limit_bytes=8 * MIB),
        name="turn_lower" if side else "turn_upper",
    )(*blocks, *turns)


def last_body(tile, count, flag_ref, done_ref, upper_ref, *refs):
    lower_refs, (high_ref, low_ref) = refs[:count], refs[count : count + 2]
    piece_refs, out_ref = refs[count + 2 : 2 * count + 2], refs[2 * count + 2]
    stage_ref, sem = refs[2 * count + 3 :]
    width = upper_ref.shape[1]
    columns = out_ref.at[:, pl.ds(0, width)]

    @pl.when(flag_ref[0] == 1)
    def _():
        fetch = pltpu.make_async_copy(done_ref, stage_ref, sem)
        fetch.start()
        fetch.wait()

    @pl.when(flag_ref[0] == 0)
    def _():
        at = 0
        for lower_ref, piece_ref in zip(lower_refs, piece_refs):
            for inner in range(0, lower_ref.shape[0], tile):
                blocks, starts = (upper_ref, lower_ref), (at - inner, 0)
                stage_ref[pl.ds(at, tile), :] = turn_rows(
                    blocks, starts, high_ref, low_ref, 0, inner, tile
                )
                piece_ref[pl.ds(inner, tile), :] = turn_rows(
                    blocks, starts, high_ref, low_ref, 1, inner, tile
                )
                at += tile

    copy = pltpu.make_async_copy(stage_ref, columns, sem)
    copy.start()
    copy.wait()


def last_turn(flag, done, upper, far, turns_far, tile=512):
    rows, width = upper.shape
    everywhere = pl.BlockSpec(memory_space=pl.ANY)
    *pieces, out = pl.pallas_call(
        functools.partial(last_body, tile, len(far)),
        in_specs=[pl.BlockSpec(memory_space=pltpu.SMEM)] + [VMEM] * (4 + len(far)),
        out_specs=(*[VMEM] * len(far), everywhere),
        out_shape=(
            *[jax.ShapeDtypeStruct(piece.shape, F32) for piece in far],
            jax.ShapeDtypeStruct((rows, 2 * width), F32),
        ),
        scratch_shapes=[pltpu.VMEM((rows, width), F32), pltpu.SemaphoreType.DMA],
        compiler_params=pltpu.CompilerParams(vmem_limit_bytes=8 * MIB),
        name="last_turn",
    )(flag, done, upper, *far, *turns_far)
    return pieces, out


def finish_body(count, flag_ref, before_ref, *refs):
    near_refs, far_refs, out_ref = refs[:count], refs[count : 2 * count], refs[2 * count]
    stage_ref, in_sems, out_sems = refs[2 * count + 1 :]
    width = stage_ref.shape[1]
    for want, sources in ((1, near_refs), (0, far_refs)):

        @pl.when(flag_ref[0] == want)
        def _(sources=sources):
            at, spans, fetches, puts = 0, [], [], []
            for k, source in enumerate(sources):
                spans.append(pl.ds(at, source.shape[0]))
                fetches.append(
                    pltpu.make_async_copy(source, stage_ref.at[spans[k], :], in_sems.at[k])
                )
                fetches[k].start()
                at += source.shape[0]
            for k, span in enumerate(spans):
                fetches[k].wait()
                place = out_ref.at[span, pl.ds(width, width)]
                puts.append(pltpu.make_async_copy(stage_ref.at[span, :], place, out_sems.at[k]))
                puts[k].start()
            for put in puts:
                put.wait()


def finish(flag, out, near, far):
    rows, width = out.shape[0], out.shape[1] // 2
    everywhere = pl.BlockSpec(memory_space=pl.ANY)
    count = len(near)
    return pl.pallas_call(
        functools.partial(finish_body, count),
        in_specs=[pl.BlockSpec(memory_space=pltpu.SMEM)] + [everywhere] * (1 + 2 * count),
        out_specs=everywhere,
        out_shape=jax.ShapeDtypeStruct(out.shape, F32),
        scratch_shapes=[
            pltpu.VMEM((rows, width), F32),
            pltpu.SemaphoreType.DMA((count,)),
            pltpu.SemaphoreType.DMA((count,)),
        ],
        input_output_aliases={1: 0},
        compiler_params=pltpu.CompilerParams(vmem_limit_bytes=8 * MIB),
        name="finish",
    )(flag, out, *near, *far)


def move(value, target):
    wide, narrow = lax.axis_size("wide"), lax.axis_size("narrow")
    pairs = []
    for w in range(wide):
        for n in range(narrow):
            to = target(w, n)
            if to is not None:
                pairs.append((w * narrow + n, (to[0] % wide) * narrow + to[1]))
    return lax.ppermute(value, ("wide", "narrow"), pairs)


def all_sum(value, active=None, rounds=ROUNDS):
    for k, mask in enumerate(rounds):
        other = move(
            value, lambda w, n: (w, n ^ mask if active is None or w % 2 == active else n)
        )
        if k + 1 == len(rounds):
            return value, other
        value = value + other


def within(w, n):
    return w ^ 1, n


def onward(w, n):
    return w + 1, n


def shards(matrix):
    rows = matrix.shape[0]
    piece, small = rows // PIECES, rows // LAST_PIECES
    starts = [k * piece for k in range(PIECES)]
    last_starts = [k * small for k in range(LAST_PIECES)]
    flag = (lax.axis_index("wide") & 1).astype(jnp.int32).reshape(1)
    turns = solve(*all_sum(first_gram(matrix)))
    near, far = [], []
    for at in starts:
        lower = turn([matrix], turns, 1, (at,), piece)
        near.append(move(lower, within))
        far.append(move(lower, onward))
    upper = turn([matrix], turns, 0, (0,), rows)
    turns = solve(*all_sum(gram(upper, near), 1, (2, 6, 1)))
    after = [
        turn([upper, near[at // piece]], turns, 1, (at, at % piece), small)
        for at in last_starts
    ]
    done = turn([upper, *near], turns, 0, None, rows)
    last_far = [move(lower, onward) for lower in after]
    parts = gram(upper, far)
    parts = parts + move(parts, lambda w, n: (w, n if w % 2 else n ^ 1))
    parts = all_sum(parts, None, (2, 6))
    turns = solve(*parts)
    pieces, out = last_turn(flag, done, upper, far, turns)
    last_near = [move(lower, within) for lower in pieces]
    return finish(flag, out, last_near, last_far)


def solution(mesh):
    spec = P("narrow", "wide")

    return jax.shard_map(shards, mesh=mesh, in_specs=(spec,), out_specs=spec, check_vma=False)
```
